128 devices in a mesh: ctx: 16 (over z_lo, x, core), tp: 8 (over z_hi, y).
Axes of the slice: x: 4, y: 4, z: 4 (z_hi: 2, z_lo: 2; z = z_hi * 2 + z_lo), core: 2. Of those that a mesh axis runs over, the one named last changes fastest.
Arguments:
- attn_q: bfloat16 [2048, 4096], P('ctx', 'tp'), may hold values from -72 to 72
- attn_k: bfloat16 [2048, 4096], P('ctx', 'tp'), may hold values from -7 to 7
- attn_v: bfloat16 [2048, 4096], P('ctx', 'tp'), may hold values from -6 to 6
- conv_x1: bfloat16 [2048, 4096], P('ctx', 'tp'), may hold values from -6 to 6
- conv_x2: bfloat16 [2048, 4096], P('ctx', 'tp'), may hold values from -6 to 6
- conv_v: bfloat16 [2048, 4096], P('ctx', 'tp'), may hold values from -6 to 6
- conv_filter: float32 [128, 256], P(None, 'tp'), may hold values from -0.5 to 0.5
- attn_proj: bfloat16 [4096, 8192], P('tp'), may hold values from -0.09375 to 0.09375
- conv_proj: bfloat16 [4096, 8192], P('tp'), may hold values from -0.09375 to 0.09375
- out_grad: bfloat16 [2048, 8192], P(('ctx', 'tp')), may hold values from -6 to 6
Outputs:
- mixed: bfloat16 [2048, 8192], P(('ctx', 'tp'))
- grad_q: bfloat16 [2048, 4096], P('ctx', 'tp')
- grad_k: bfloat16 [2048, 4096], P('ctx', 'tp')
- grad_v: bfloat16 [2048, 4096], P('ctx', 'tp')
- grad_x1: bfloat16 [2048, 4096], P('ctx', 'tp')
- grad_x2: bfloat16 [2048, 4096], P('ctx', 'tp')
- grad_conv_v: bfloat16 [2048, 4096], P('ctx', 'tp')
- filter_grad: float32 [128, 256], P(None, 'tp')
The draws below stay inside these ranges and needn't reach their ends.
All inputs are finite; a program needn't handle non-finite values.
Results may differ from the reference program's by a relative error of at most 0.03.
Values may be sent and summed in bfloat16 or wider, within the bound.
No kernel may reach another device: no remote copies, remote signals or barrier semaphores. Data moves between devices by JAX's collectives and lax.ppermute only.
A program may use at most 128 MiB of HBM per device.

```python
import math
import jax
import jax.numpy as jnp
from jax import lax

D = 8192
HEADS = 32
HEAD = 128
HCH = 4096
GSIZE = 16
TAPS = 128
LENGTH = 2048
HGROUPS = 256


def query_key_pair(key):
    base = jax.random.fold_in(key, 11)
    first, second = jax.random.split(base)
    shape = (LENGTH, HEADS * HEAD)
    queries = jnp.clip(1.7 * jax.random.normal(first, shape, jnp.float32), -7.0, 7.0)
    keys = jnp.clip(1.7 * jax.random.normal(second, shape, jnp.float32), -7.0, 7.0)
    return (queries, keys)


def draw_attn_q(key, part):
    return query_key_pair(key)[0].astype(jnp.bfloat16)


def draw_attn_k(key, part):
    return query_key_pair(key)[1].astype(jnp.bfloat16)


def block_scale(key, dims, cuts, smallest, top_value):
    def one(dim, blocks):
        heights = jax.random.uniform(jax.random.fold_in(jax.random.fold_in(key, 6), dim), (blocks,), jnp.float32, smallest / len(cuts), top_value / len(cuts))
        return jnp.repeat(jnp.exp(heights), dims[dim] // blocks).reshape((-1,) + (1,) * (len(dims) - dim - 1))

    gain = one(*cuts[0])
    for cut in cuts[1:]:
        gain = gain * one(*cut)
    return gain


def noise(own_key, extent, deviation, bound, pieces=(), held_as=jnp.bfloat16):
    level = block_scale(own_key, extent, pieces, -0.22, 0.18) if pieces else 1.0
    entries = jax.random.normal(own_key, extent, jnp.float32) * deviation * level
    return jnp.minimum(jnp.maximum(entries, -bound), bound).astype(held_as)


def setup_inputs(seed: int = 0) -> dict:
    splits = jax.random.split(jax.random.key(seed), 11)
    attn_q = draw_attn_q(jax.random.fold_in(splits[10], 71), 0)
    attn_k = draw_attn_k(jax.random.fold_in(splits[10], 71), 0)
    attn_v = noise(splits[2], (LENGTH, HEADS * HEAD), 1.0, 6.0, ((0, 16), (1, 8)))
    conv_x1 = noise(splits[3], (LENGTH, HCH), 1.0, 6.0, ((0, 16), (1, 8)))
    conv_x2 = noise(splits[4], (LENGTH, HCH), 1.0, 6.0, ((0, 16), (1, 8)))
    conv_v = noise(splits[5], (LENGTH, HCH), 1.0, 6.0, ((0, 16), (1, 8)))
    conv_filter = noise(splits[6], (TAPS, HGROUPS), 0.09, 0.5, ((1, 8),), jnp.float32)
    attn_proj = noise(splits[7], (HEADS * HEAD, D), (HEADS * HEAD) ** -0.5, 0.09375, ((0, 8),))
    conv_proj = noise(splits[8], (HCH, D), HCH ** -0.5, 0.09375, ((0, 8),))
    out_grad = noise(splits[9], (LENGTH, D), 1.0, 6.0, ((0, 128),))
    return {"attn_q": attn_q, "attn_k": attn_k, "attn_v": attn_v, "conv_x1": conv_x1, "conv_x2": conv_x2, "conv_v": conv_v, "conv_filter": conv_filter, "attn_proj": attn_proj, "conv_proj": conv_proj, "out_grad": out_grad}


def split_heads(matrix):
    return matrix.reshape(LENGTH, HEADS, HEAD).transpose(1, 0, 2)

def merge_heads(stacked):
    return stacked.transpose(1, 0, 2).reshape(LENGTH, HEADS * HEAD)

def attend(inputs):
    queries, keys, values = inputs
    block = min(512, LENGTH)
    scale = 1.0 / math.sqrt(HEAD)
    key_pos = jnp.arange(LENGTH, dtype=jnp.int32)

    def one_block(index):
        rows = lax.dynamic_slice_in_dim(queries, (index * block).astype(jnp.int32), block, 0)
        query_pos = index * block + jnp.arange(block, dtype=jnp.int32)
        scores = jnp.dot(rows, keys.T, preferred_element_type=jnp.float32) * scale
        scores = jnp.where(key_pos[None, :] <= query_pos[:, None], scores, -jnp.inf)
        peak = lax.optimization_barrier(jnp.max(scores, axis=-1))
        weights = jnp.exp(scores - peak[:, None])
        norm = lax.optimization_barrier(jnp.sum(weights, axis=-1))
        output = jnp.dot(weights.astype(jnp.bfloat16), values, preferred_element_type=jnp.float32) / norm[:, None]
        return (output.astype(jnp.bfloat16), peak + jnp.log(norm))
    outputs, totals = lax.map(one_block, jnp.arange(LENGTH // block, dtype=jnp.int32))
    return (outputs.reshape(LENGTH, HEAD), totals.reshape(LENGTH))

def attend_back(inputs):
    queries, keys, values, output, grad_out, log_total = inputs
    block = min(512, LENGTH)
    scale = 1.0 / math.sqrt(HEAD)
    key_pos = jnp.arange(LENGTH, dtype=jnp.int32)
    delta = lax.optimization_barrier(jnp.sum(grad_out.astype(jnp.float32) * output.astype(jnp.float32), axis=-1))

    def one_block(carry, index):
        grad_k, grad_v = carry
        begin = (index * block).astype(jnp.int32)
        rows = lax.dynamic_slice_in_dim(queries, begin, block, 0)
        grads = lax.dynamic_slice_in_dim(grad_out, begin, block, 0)
        totals = lax.dynamic_slice_in_dim(log_total, begin, block, 0)
        deltas = lax.dynamic_slice_in_dim(delta, begin, block, 0)
        query_pos = index * block + jnp.arange(block, dtype=jnp.int32)
        scores = jnp.dot(rows, keys.T, preferred_element_type=jnp.float32) * scale
        scores = jnp.where(key_pos[None, :] <= query_pos[:, None], scores, -jnp.inf)
        probs = jnp.exp(scores - totals[:, None])
        grad_v = grad_v + jnp.dot(probs.astype(jnp.bfloat16).T, grads, preferred_element_type=jnp.float32)
        grad_p = jnp.dot(grads, values.T, preferred_element_type=jnp.float32)
        grad_s = (probs * (grad_p - deltas[:, None])).astype(jnp.bfloat16)
        grad_q = jnp.dot(grad_s, keys, preferred_element_type=jnp.float32) * scale
        grad_k = grad_k + jnp.dot(grad_s.T, rows, preferred_element_type=jnp.float32) * scale
        return ((grad_k, grad_v), grad_q.astype(jnp.bfloat16))
    start = (jnp.zeros((LENGTH, HEAD), jnp.float32), jnp.zeros((LENGTH, HEAD), jnp.float32))
    (grad_k, grad_v), grad_q = lax.scan(one_block, start, jnp.arange(LENGTH // block, dtype=jnp.int32))
    return (grad_q.reshape(LENGTH, HEAD), grad_k.astype(jnp.bfloat16), grad_v.astype(jnp.bfloat16))

def reference(attn_q, attn_k, attn_v, conv_x1, conv_x2, conv_v, conv_filter, attn_proj, conv_proj, out_grad):
    head_q, head_k, head_v = (split_heads(attn_q), split_heads(attn_k), split_heads(attn_v))
    outputs, log_total = lax.map(attend, (head_q, head_k, head_v))
    attention = merge_heads(outputs)
    product = (conv_x1.astype(jnp.float32) * conv_v.astype(jnp.float32)).astype(jnp.bfloat16)
    taps_full = jnp.repeat(conv_filter, GSIZE, axis=1)
    padded = jnp.concatenate([jnp.zeros((TAPS - 1, HCH), jnp.bfloat16), product], axis=0)

    def conv_step(index, total):
        window = lax.dynamic_slice_in_dim(padded, (TAPS - 1 - index).astype(jnp.int32), LENGTH, 0)
        return total + taps_full[index][None, :] * window.astype(jnp.float32)
    filtered = lax.fori_loop(jnp.int32(0), jnp.int32(TAPS), conv_step, jnp.zeros((LENGTH, HCH), jnp.float32))
    gated = (conv_x2.astype(jnp.float32) * filtered).astype(jnp.bfloat16)
    mixed = (jnp.dot(attention, attn_proj, preferred_element_type=jnp.float32) + jnp.dot(gated, conv_proj, preferred_element_type=jnp.float32)).astype(jnp.bfloat16)
    contract = (((1,), (1,)), ((), ()))
    grad_attention = lax.dot_general(out_grad, attn_proj, contract, preferred_element_type=jnp.float32).astype(jnp.bfloat16)
    grad_gated = lax.dot_general(out_grad, conv_proj, contract, preferred_element_type=jnp.float32)
    grad_x2 = (grad_gated * filtered).astype(jnp.bfloat16)
    grad_filtered = (grad_gated * conv_x2.astype(jnp.float32)).astype(jnp.bfloat16)
    padded_after = jnp.concatenate([grad_filtered, jnp.zeros((TAPS - 1, HCH), jnp.bfloat16)], axis=0)

    def back_step(index, total):
        window = lax.dynamic_slice_in_dim(padded_after, index.astype(jnp.int32), LENGTH, 0)
        return total + taps_full[index][None, :] * window.astype(jnp.float32)
    grad_product = lax.fori_loop(jnp.int32(0), jnp.int32(TAPS), back_step, jnp.zeros((LENGTH, HCH), jnp.float32))
    grad_x1 = (grad_product * conv_v.astype(jnp.float32)).astype(jnp.bfloat16)
    grad_conv_v = (grad_product * conv_x1.astype(jnp.float32)).astype(jnp.bfloat16)

    def tap_grad(index):
        window = lax.dynamic_slice_in_dim(padded, (TAPS - 1 - index).astype(jnp.int32), LENGTH, 0)
        return lax.optimization_barrier(jnp.sum(grad_filtered.astype(jnp.float32) * window.astype(jnp.float32), axis=0))
    local_grad = lax.map(tap_grad, jnp.arange(TAPS, dtype=jnp.int32))
    filter_grad = local_grad.reshape(TAPS, HGROUPS, GSIZE).sum(axis=-1) / math.sqrt(LENGTH * GSIZE)
    head_grad = split_heads(grad_attention)
    grad_q, grad_k, grad_v = lax.map(attend_back, (head_q, head_k, head_v, outputs, head_grad, log_total))
    return (mixed, merge_heads(grad_q), merge_heads(grad_k), merge_heads(grad_v), grad_x1, grad_x2, grad_conv_v, filter_grad)
```

```python
import functools
import math

import jax
import jax.numpy as jnp
from jax import lax
from jax.experimental import pallas as pl
from jax.experimental.pallas import tpu as pltpu
from jax.sharding import PartitionSpec as P

HEAD = 128
GSIZE = 16
F32 = jnp.float32
BF16 = jnp.bfloat16
NT = (((1,), (1,)), ((), ()))
TN = (((0,), (0,)), ((), ()))
SCALE = 1.0 / math.sqrt(HEAD)
NEG = -1e30


def vmem():
    return pl.BlockSpec(memory_space=pltpu.VMEM)


def hbm():
    return pl.BlockSpec(memory_space=pl.ANY)


def shape(dims, dtype=BF16):
    return jax.ShapeDtypeStruct(dims, dtype)


def cost(flops, nbytes):
    return pl.CostEstimate(flops=int(flops), bytes_accessed=int(nbytes), transcendentals=0)


def call(body, args, outs, scratch=(), in_specs=None, flops=1e8, nbytes=1 << 20, limit=None):
    params = pltpu.CompilerParams(vmem_limit_bytes=limit) if limit else None
    return pl.pallas_call(
        body,
        in_specs=in_specs or [vmem() for _ in args],
        out_specs=[vmem() for _ in outs],
        out_shape=list(outs),
        scratch_shapes=list(scratch),
        compiler_params=params,
        cost_estimate=cost(flops, nbytes),
    )(*args)


def ctx_place():
    i = lax.axis_index("ctx")
    return (i // 8) * 2 + i % 2, (i // 2) % 4


def quad_perm(j):
    pairs = []
    for z in range(2):
        for x in range(4):
            for c in range(2):
                pairs.append((z * 8 + x * 2 + c, (z ^ (j >> 1)) * 8 + x * 2 + (c ^ (j & 1))))
    return pairs


def x_perm(k):
    return [(z * 8 + x * 2 + c, z * 8 + ((x + k) % 4) * 2 + c) for z in range(2) for x in range(4) for c in range(2)]


def tp_perm(j):
    dz, dy = j >> 2, j & 3
    return [(z * 4 + y, ((z + dz) % 2) * 4 + (y + dy) % 4) for z in range(2) for y in range(4)]


def tp_to(j):
    i = lax.axis_index("tp")
    return lax.rem(i // 4 + (j >> 2), 2) * 4 + lax.rem(i % 4 + (j & 3), 4)


def tp_from(j):
    i = lax.axis_index("tp")
    return lax.rem(i // 4 + (j >> 2), 2) * 4 + lax.rem(i % 4 + 4 - (j & 3), 4)


def lane(head):
    return pl.ds(pl.multiple_of(head * HEAD, HEAD), HEAD)


def rows(index, size):
    return pl.ds(pl.multiple_of(index * size, size), size)


def pack_body(q, k, v, *outs):
    quad, _ = ctx_place()
    for j in range(4):
        at = lane(quad ^ j)
        outs[j][:, :128] = q[:, at]
        outs[j][:, 128:256] = k[:, at]
        outs[j][:, 256:] = v[:, at]


def fwd_body(p0, p1, p2, p3, g1, g2, g3, o0, o1, o2, o3, qn, kn, vn, on, lse):
    quad, x = ctx_place()
    for j, piece in enumerate((p0, p1, p2, p3)):
        at = quad ^ j
        qn[rows(at, 128), :] = piece[:, :128]
        to = pl.ds(pl.multiple_of((at // 2) * 1024 + x * 256 + (at % 2) * 128, 128), 128)
        kn[to, :] = piece[:, 128:256]
        vn[to, :] = piece[:, 256:]
    for k, got in ((1, g1), (2, g2), (3, g3)):
        src = lax.rem(x + 4 - k, 4)
        for j in range(4):
            at = quad ^ j
            to = pl.ds(pl.multiple_of((at // 2) * 1024 + src * 256 + (at % 2) * 128, 128), 128)
            kn[to, :] = got[j * 128 : (j + 1) * 128, :128]
            vn[to, :] = got[j * 128 : (j + 1) * 128, 128:]
    sub = 128
    for r in range(512 // sub):
        q = qn[r * sub : (r + 1) * sub, :]
        upper = (r * sub) // 256
        offset = x * 256 + (r * sub) % 256
        qpos = offset + lax.broadcasted_iota(jnp.int32, (sub, 1024), 0)
        kpos = lax.broadcasted_iota(jnp.int32, (sub, 1024), 1)
        visible = kpos <= qpos
        parts = []
        for half in range(upper + 1):
            s = lax.dot_general(q, kn[half * 1024 : (half + 1) * 1024, :], NT, preferred_element_type=F32) * SCALE
            parts.append(jnp.where(visible, s, NEG) if half == upper else s)
        peak = jnp.max(parts[0], axis=1, keepdims=True)
        for s in parts[1:]:
            peak = jnp.maximum(peak, jnp.max(s, axis=1, keepdims=True))
        norm = jnp.zeros((sub, 1), F32)
        total = jnp.zeros((sub, HEAD), F32)
        for half, s in enumerate(parts):
            w = jnp.exp(s - peak)
            norm = norm + jnp.sum(w, axis=1, keepdims=True)
            total = total + jnp.dot(w.astype(BF16), vn[half * 1024 : (half + 1) * 1024, :], preferred_element_type=F32)
        on[r * sub : (r + 1) * sub, :] = (total / norm).astype(BF16)
        lse[r * sub : (r + 1) * sub, :] = jnp.broadcast_to(peak + jnp.log(norm), (sub, HEAD))
    for j, o in enumerate((o0, o1, o2, o3)):
        o[...] = on[rows(quad ^ j, 128), :]


def bwd_body(d0, d1, d2, d3, qn, kn, vn, on, lse, dq, e0, e1, e2, e3, dn, dk, dv):
    quad, x = ctx_place()
    for j, d in enumerate((d0, d1, d2, d3)):
        dn[rows(quad ^ j, 128), :] = d[...]
    for upper in range(2):
        q = qn[upper * 256 : (upper + 1) * 256, :]
        d = dn[upper * 256 : (upper + 1) * 256, :]
        o = on[upper * 256 : (upper + 1) * 256, :]
        total = lse[upper * 256 : (upper + 1) * 256, :1]
        delta = jnp.sum(d.astype(F32) * o.astype(F32), axis=1, keepdims=True)
        acc = jnp.zeros((256, HEAD), F32)
        for half in range(upper + 1):
            at = slice(half * 1024, (half + 1) * 1024)
            k = kn[at, :]
            v = vn[at, :]
            s = lax.dot_general(q, k, NT, preferred_element_type=F32) * SCALE
            p = jnp.exp(s - total)
            if half == upper:
                qpos = x * 256 + lax.broadcasted_iota(jnp.int32, (256, 1024), 0)
                kpos = lax.broadcasted_iota(jnp.int32, (256, 1024), 1)
                p = jnp.where(kpos <= qpos, p, 0.0)
            gp = lax.dot_general(d, v, NT, preferred_element_type=F32)
            ds = (p * (gp - delta)).astype(BF16)
            pv = lax.dot_general(p.astype(BF16), d, TN, preferred_element_type=F32)
            pk = lax.dot_general(ds, q, TN, preferred_element_type=F32) * SCALE
            if upper == 1 and half == 0:
                dk[at, :] = dk[at, :] + pk
                dv[at, :] = dv[at, :] + pv
            else:
                dk[at, :] = pk
                dv[at, :] = pv
            acc = acc + jnp.dot(ds, k, preferred_element_type=F32)
        dq[upper * 256 : (upper + 1) * 256, :] = (acc * SCALE).astype(BF16)
    for k, e in enumerate((e0, e1, e2, e3)):
        to = lax.rem(x + k, 4)
        for z in range(2):
            at = pl.ds(pl.multiple_of(z * 1024 + to * 256, 256), 256)
            e[z * 256 : (z + 1) * 256, :128] = dk[at, :].astype(BF16)
            e[z * 256 : (z + 1) * 256, 128:] = dv[at, :].astype(BF16)


def sum_body(e0, m1, m2, m3, dq, f0, f1, f2, f3, t0, t1, t2, t3, fs):
    quad, x = ctx_place()
    for k, f in enumerate((f0, f1, f2, f3)):
        fs[rows(lax.rem(x + 4 - k, 4), 32), :] = f[:, :128].astype(F32) + f[:, 128:].astype(F32)
    grad = (fs[0:32, :] + fs[32:64, :]) + (fs[64:96, :] + fs[96:128, :])
    high = grad.astype(BF16)
    low = (grad - high.astype(F32)).astype(BF16)
    for j, t in enumerate((t0, t1, t2, t3)):
        at = rows(quad ^ j, 128)
        t[:128, :128] = dq[at, :]
        t[:128, 128:] = (
            e0[at, :].astype(F32) + m1[at, :].astype(F32) + m2[at, :].astype(F32) + m3[at, :].astype(F32)
        ).astype(BF16)
        t[128:, :128] = high
        t[128:, 128:256] = low
        t[128:, 256:] = jnp.zeros((32, 128), BF16)


def final_body(t0, u1, u2, u3, dq, dk, dv, fg, fs, *, fscale):
    quad, _ = ctx_place()
    for j, t in enumerate((t0, u1, u2, u3)):
        at = lane(quad ^ j)
        dq[:, at] = t[:128, :128]
        dk[:, at] = t[:128, 128:256]
        dv[:, at] = t[:128, 256:]
        fs[rows(quad ^ j, 32), :] = t[128:, :128].astype(F32) + t[128:, 128:256].astype(F32)
    grad = (fs[0:32, :] + fs[32:64, :]) + (fs[64:96, :] + fs[96:128, :])
    fg[...] = grad.T * fscale


def mix_body(a0, a1, a2, a3, gated, wa, wc, *rest):
    outs, act, full = rest[:8], rest[8], rest[9]

    @pl.when(pl.program_id(0) == 0)
    def _():
        quad, _ = ctx_place()
        for j, a in enumerate((a0, a1, a2, a3)):
            full[:, lane(quad ^ j)] = a[...]
        for j in range(8):
            at = rows(tp_to(j), 16)
            act[j * 16 : (j + 1) * 16, :512] = full[at, :]
            act[j * 16 : (j + 1) * 16, 512:] = gated[at, :]

    part = jnp.dot(act[:, :512], wa[...], preferred_element_type=F32)
    part = part + jnp.dot(act[:, 512:], wc[...], preferred_element_type=F32)
    for j in range(8):
        outs[j][...] = part[j * 16 : (j + 1) * 16, :].astype(BF16)


def mix(pieces, gated, wa, wc):
    width = wa.shape[1]
    tile = 2048
    keep = lambda r, c: pl.BlockSpec((r, c), lambda i: (0, 0))
    return pl.pallas_call(
        mix_body,
        grid=(width // tile,),
        in_specs=[keep(128, 128)] * 4
        + [keep(128, 512), pl.BlockSpec((512, tile), lambda i: (0, i)), pl.BlockSpec((512, tile), lambda i: (0, i))],
        out_specs=[pl.BlockSpec((16, tile), lambda i: (0, i))] * 8,
        out_shape=[shape((16, width))] * 8,
        scratch_shapes=[pltpu.VMEM((128, 1024), BF16), pltpu.VMEM((128, 512), BF16)],
        cost_estimate=cost(4e9, 20 << 20),
    )(*pieces, gated, wa, wc)


def load_rows(pieces, full, sems):
    copies = []
    for j, piece in enumerate(pieces):
        copy = pltpu.make_async_copy(piece, full.at[rows(tp_from(j), 16), :], sems.at[j])
        copy.start()
        copies.append(copy)
    return copies


CHUNKS = 8


def project(pieces, w, full, wbuf, acc, sems, wsems):
    step = w.shape[1] // CHUNKS
    copies = load_rows(pieces, full, sems)
    wcopies = []
    for c in range(CHUNKS):
        at = slice(c * step, (c + 1) * step)
        copy = pltpu.make_async_copy(w.at[:, at], wbuf.at[:, at], wsems.at[c])
        copy.start()
        wcopies.append(copy)
    for copy in copies:
        copy.wait()
    for c in range(CHUNKS):
        at = slice(c * step, (c + 1) * step)
        wcopies[c].wait()
        part = lax.dot_general(full[:, at], wbuf[:, at], NT, preferred_element_type=F32)
        if c == 0:
            acc[...] = part
        else:
            acc[...] = acc[...] + part


def attn_proj_body(*refs):
    pieces, w, outs, scratch = refs[:8], refs[8], refs[9:13], refs[13:]
    full, wbuf, acc, sems, wsems = scratch
    project(pieces, w, full, wbuf, acc, sems, wsems)
    quad, _ = ctx_place()
    for j in range(4):
        outs[j][...] = acc[:, lane(quad ^ j)].astype(BF16)


def conv_proj_body(*refs):
    pieces, w, x2, filtered, gf, gx2 = refs[:8], refs[8], refs[9], refs[10], refs[11], refs[12]
    full, wbuf, acc, sems, wsems = refs[13:]
    project(pieces, w, full, wbuf, acc, sems, wsems)
    grad = acc[...]
    gf[...] = (grad * x2[...].astype(F32)).astype(BF16)
    gx2[...] = (grad * filtered[...]).astype(BF16)


def proj_scratch():
    return [
        pltpu.VMEM((128, 8192), BF16),
        pltpu.VMEM((512, 8192), BF16),
        pltpu.VMEM((128, 512), F32),
        pltpu.SemaphoreType.DMA((8,)),
        pltpu.SemaphoreType.DMA((CHUNKS,)),
    ]


def banded(base, g):
    row = jnp.broadcast_to(base[g : g + 1, :], (128, 256))
    return pltpu.roll(row, 0, 1, stride=1, stride_axis=0).astype(BF16)


def grouped(base, wide, tile):
    source = wide[:, tile * 128 : (tile + 1) * 128]
    group = lax.broadcasted_iota(jnp.int32, (128, 128), 1) // GSIZE
    result = jnp.zeros((128, 128), F32)
    for g in range(8):
        part = jnp.dot(banded(base, tile * 8 + g), source, preferred_element_type=F32)
        result = jnp.where(group == g, part, result)
    return result


def conv_fwd_body(halo, product, x2, base, filtered, gated, wide):
    wide[:128, :] = halo[...]
    wide[128:, :] = product[...]
    for tile in range(4):
        at = slice(tile * 128, (tile + 1) * 128)
        result = grouped(base, wide, tile)
        filtered[:, at] = result
        gated[:, at] = (x2[:, at].astype(F32) * result).astype(BF16)


def conv_bwd_body(gf, halo_after, halo, product, x1, v, base, gx1, gv, fgrad, wide, before, corr):
    wide[:128, :] = gf[...]
    wide[128:, :] = halo_after[...]
    before[:128, :] = halo[...]
    before[128:, :] = product[...]
    group = lax.broadcasted_iota(jnp.int32, (128, 128), 1) // GSIZE
    mirror = lax.broadcasted_iota(jnp.int32, (128, 128), 0) + lax.broadcasted_iota(jnp.int32, (128, 128), 1)
    mirrored = jnp.dot(jnp.where(mirror == 127, 1.0, 0.0).astype(BF16), gf[...], preferred_element_type=F32)
    for tile in range(4):
        at = slice(tile * 128, (tile + 1) * 128)
        result = grouped(base, wide, tile)
        gx1[:, at] = (result * v[:, at].astype(F32)).astype(BF16)
        gv[:, at] = (result * x1[:, at].astype(F32)).astype(BF16)
        source = before[:, at]
        grad = mirrored[:, at]
        for g in range(8):
            own = jnp.where(group == g, grad, 0.0).astype(BF16)
            cross = lax.dot_general(own, source, NT, preferred_element_type=F32)
            cross = pltpu.roll(cross, 129, 1, stride=1, stride_axis=0)
            corr[tile * 8 + g : tile * 8 + g + 1, :] = jnp.sum(cross, axis=0, keepdims=True)
    lanes = lax.broadcasted_iota(jnp.int32, (256, 128), 0) + lax.broadcasted_iota(jnp.int32, (256, 128), 1)
    flip = jnp.where(lanes == 128, 1.0, 0.0).astype(F32)
    grad = jnp.dot(corr[...], flip, preferred_element_type=F32, precision=lax.Precision.HIGHEST)
    high = grad.astype(BF16)
    fgrad[:, :128] = high
    fgrad[:, 128:] = (grad - high.astype(F32)).astype(BF16)


def local(attn_q, attn_k, attn_v, conv_x1, conv_x2, conv_v, conv_filter, attn_proj, conv_proj, out_grad):
    seq = attn_q.shape[0] * lax.axis_size("ctx")
    send = lambda a, pairs, axis="ctx": lax.ppermute(a, axis, pairs)
    pieces = [out_grad] + [send(out_grad, tp_perm(j), "tp") for j in range(1, 8)]
    packs = call(pack_body, (attn_q, attn_k, attn_v), [shape((128, 384))] * 4)
    mine = [packs[0]] + [send(packs[j], quad_perm(j)) for j in range(1, 4)]
    rows_kv = jnp.concatenate([m[:, 128:] for m in mine], axis=0)
    along = [send(rows_kv, x_perm(k)) for k in range(1, 4)]
    product = (conv_x1.astype(F32) * conv_v.astype(F32)).astype(BF16)
    halo = send(product, [(i, i + 1) for i in range(15)])
    taps = conv_filter.T
    forward_base = jnp.pad(taps[:, ::-1], ((0, 0), (1, 127)))
    backward_base = jnp.pad(taps, ((0, 0), (0, 128)))
    filtered, gated = call(
        conv_fwd_body,
        (halo, product, conv_x2, forward_base),
        [shape((128, 512), F32), shape((128, 512))],
        [pltpu.VMEM((256, 512), BF16)],
        flops=1e9,
    )
    res = call(
        fwd_body,
        (*mine, *along),
        [shape((128, 128))] * 4
        + [shape((512, 128)), shape((2048, 128)), shape((2048, 128)), shape((512, 128)), shape((512, 128), F32)],
        flops=2e9,
    )
    heads, (qn, kn, vn, on, lse) = res[:4], res[4:]
    attention = [heads[0]] + [send(heads[j], quad_perm(j)) for j in range(1, 4)]
    parts = mix(attention, gated, attn_proj, conv_proj)
    got = [parts[0]] + [send(parts[j], tp_perm(j), "tp") for j in range(1, 8)]
    mixed = functools.reduce(lambda a, b: a + b, [g.astype(F32) for g in got]).astype(BF16)
    specs = [hbm()] * 9
    grads = call(
        attn_proj_body, (*pieces, attn_proj), [shape((128, 128))] * 4, proj_scratch(), specs, flops=4e9, nbytes=10 << 20
    )
    d = [grads[0]] + [send(grads[j], quad_perm(j)) for j in range(1, 4)]
    gf, grad_x2 = call(
        conv_proj_body,
        (*pieces, conv_proj, conv_x2, filtered),
        [shape((128, 512)), shape((128, 512))],
        proj_scratch(),
        specs + [vmem(), vmem()],
        flops=4e9,
        nbytes=10 << 20,
    )
    halo_after = send(gf, [(i + 1, i) for i in range(15)])
    dq, e0, e1, e2, e3 = call(
        bwd_body,
        (*d, qn, kn, vn, on, lse),
        [shape((512, 128))] + [shape((512, 256))] * 4,
        [pltpu.VMEM((512, 128), BF16), pltpu.VMEM((2048, 128), F32), pltpu.VMEM((2048, 128), F32)],
        flops=4e9,
    )
    m = [e0] + [send(e, x_perm(k + 1)) for k, e in enumerate((e1, e2, e3))]
    grad_x1, grad_conv_v, fgrad = call(
        conv_bwd_body,
        (gf, halo_after, halo, product, conv_x1, conv_v, backward_base),
        [shape((128, 512)), shape((128, 512)), shape((32, 256))],
        [pltpu.VMEM((256, 512), BF16), pltpu.VMEM((256, 512), BF16), pltpu.VMEM((32, 256), F32)],
        flops=2e9,
    )
    f = [fgrad] + [send(fgrad, x_perm(k)) for k in range(1, 4)]
    t = call(sum_body, (*m, dq, *f), [shape((160, 384))] * 4, [pltpu.VMEM((128, 128), F32)])
    u = [t[0]] + [send(t[j], quad_perm(j)) for j in range(1, 4)]
    grad_q, grad_k, grad_v, filter_grad = call(
        functools.partial(final_body, fscale=1.0 / math.sqrt(seq * GSIZE)),
        tuple(u),
        [shape((128, 512))] * 3 + [shape((128, 32), F32)],
        [pltpu.VMEM((128, 128), F32)],
    )
    return (mixed, grad_q, grad_k, grad_v, grad_x1, grad_x2, grad_conv_v, filter_grad)


def solution(mesh):
    block = P("ctx", "tp")
    in_specs = (block,) * 6 + (P(None, "tp"), P("tp", None), P("tp", None), P(("ctx", "tp"), None))
    out_specs = (P(("ctx", "tp"), None),) + (block,) * 6 + (P(None, "tp"),)
    return jax.shard_map(local, mesh=mesh, in_specs=in_specs, out_specs=out_specs, check_vma=False)
```
